32 devices in a mesh: grp: 4 (over y, x), lm: 8 (over z, core).
Axes of the slice: x: 2, y: 2, z: 4, core: 2. Of those that a mesh axis runs over, the one named last changes fastest.
Arguments:
- embeddings: bfloat16 [8192, 512], P(('grp', 'lm')), may hold values from -14 to 14
- landmarks: bfloat16 [16384, 512], P('lm'), may hold values from -14 to 14
- start_vectors: float32 [8192, 128], P(('grp', 'lm')), may hold values from -10 to 10
- row_weight: float32 [8192], P(('grp', 'lm')), may hold values from 0.1 to 9
- spread: float32 [1], replicated, may hold values from 11.313708 to 33.941124
Outputs:
- subspace: float32 [8192, 128], P(('grp', 'lm'))
The draws below stay inside these ranges and needn't reach their ends.
All inputs are finite; a program needn't handle non-finite values.
Results may differ from the reference program's by a relative error of at most 0.019.
Values may be sent and summed in bfloat16 or wider, within the bound.
A program may use at most 128 MiB of HBM per device.

```python
import math
import jax
import jax.numpy as jnp
from jax import lax

D = 512
VECS = 128
ITERS = 2
ROWS = 8192
LANDMARKS = 16384


def draw_row_weight(key, part):
    position = jnp.arange(ROWS, dtype=jnp.float32) / ROWS
    base = jnp.exp(jax.random.uniform(key, (ROWS,), jnp.float32, math.log(0.1), 0.0))
    ramp = jnp.exp(position * math.log(3.0))
    return base * ramp


def feature_rows(key, count, salt):
    inner = jax.random.fold_in(key, salt)
    return jnp.clip(jax.random.normal(inner, (count, D), jnp.float32), -6.0, 6.0)


def draw_embeddings(key, part):
    return feature_rows(key, ROWS, 101).astype(jnp.bfloat16)


def draw_landmarks(key, part):
    return feature_rows(key, LANDMARKS, 202).astype(jnp.bfloat16)


def draw_start_vectors(key, part):
    first, second, third = jax.random.split(jax.random.fold_in(key, 17), 3)
    position = jnp.arange(ROWS, dtype=jnp.float32) / ROWS
    magnitude = jax.random.uniform(second, (1, VECS), jnp.float32, 1.0, 2.0)
    sign = 2.0 * jax.random.randint(third, (1, VECS), 0, 2).astype(jnp.float32) - 1.0
    column_factor = magnitude * sign
    noise = jnp.clip(jax.random.normal(first, (ROWS, VECS), jnp.float32), -6.0, 6.0)
    ramp = 0.5 * jnp.exp(position * math.log(3.0))
    return noise + ramp[:, None] * column_factor


def setup_inputs(seed: int = 0) -> dict:
    key_list = jax.random.split(jax.random.key(seed), 6)
    return {
        "embeddings": draw_embeddings(jax.random.fold_in(key_list[5], 71), 0),
        "landmarks": draw_landmarks(jax.random.fold_in(key_list[5], 71), 0),
        "start_vectors": draw_start_vectors(jax.random.fold_in(key_list[5], 71), 0),
        "row_weight": draw_row_weight(jax.random.fold_in(key_list[5], 71), 0),
        "spread": jnp.clip(jnp.exp(jax.random.uniform(key_list[4], (1,), jnp.float32, math.log(11.313708), math.log(33.941124))), 11.313708, 33.941124),
    }


def unit_rows(values):
    values = values.astype(jnp.float32)
    scale = lax.rsqrt(lax.optimization_barrier(jnp.sum(values * values, axis=1, keepdims=True)) + 1e-06)
    return (values * scale).astype(jnp.bfloat16)

def round_trip(values):
    rounded = lax.optimization_barrier(values.astype(jnp.bfloat16))
    return rounded.astype(jnp.float32)

def reference(embeddings, landmarks, start_vectors, row_weight, spread):
    highest = lax.Precision.HIGHEST
    rows_unit = unit_rows(embeddings).astype(jnp.float32)
    marks_unit = unit_rows(landmarks).astype(jnp.float32)
    total_rows = embeddings.shape[0]
    block = math.gcd(LANDMARKS, 1024)
    marks_blocks = marks_unit.reshape(LANDMARKS // block, block, D)
    gamma = spread[0]
    weight = row_weight.astype(jnp.float32)
    weight_sum = jnp.sum(weight)
    vectors = start_vectors.astype(jnp.float32)
    for step in range(ITERS):
        weighted_full = weight[:, None] * vectors
        weighted = round_trip(weighted_full)
        totals = lax.optimization_barrier(jnp.sum(weighted_full, axis=0))

        def visit(carry, marks):
            raw, shift = carry
            cosine = jnp.dot(rows_unit, marks.T, precision=highest)
            values = jnp.exp(gamma * cosine)
            kernel = round_trip(values)
            means = jnp.dot(weight, values, precision=highest) / weight_sum
            side = jnp.dot(kernel.T, weighted, precision=highest) - means[:, None] * totals[None, :]
            side_b = round_trip(side)
            raw = raw + jnp.dot(kernel, side_b, precision=highest)
            shift = shift + jnp.dot(means, side_b, precision=highest)
            return ((raw, shift), None)
        init = (jnp.zeros((total_rows, VECS), jnp.float32), jnp.zeros((VECS,), jnp.float32))
        (raw, shift), _ = lax.scan(visit, init, marks_blocks)
        image = weight[:, None] * (raw - shift[None, :])
        scale = jnp.sqrt(lax.optimization_barrier(jnp.mean(image * image, axis=0)) + 1e-06)
        vectors = image / scale[None, :]
    return vectors
```

```python
import functools

import jax
import jax.numpy as jnp
from jax import lax
from jax.experimental import pallas as pl
from jax.experimental.pallas import tpu as pltpu
from jax.sharding import PartitionSpec as P

ITERS = 2
F32 = jnp.float32
BF16 = jnp.bfloat16
HIGHEST = lax.Precision.HIGHEST


def nt(a, b):
    return lax.dot_general(a, b, (((1,), (1,)), ((), ())), preferred_element_type=F32)


def nn(a, b):
    return jnp.dot(a, b, preferred_element_type=F32)


def tile(total, most):
    size = min(total, most)
    while total % size:
        size -= 8
    return size


def rows_at(index, size):
    return pl.ds(pl.multiple_of(index * size, size), size)


def kernel(
    groups, members, spread_ref, emb_ref, marks_ref, vec_ref, weight_ref, out_ref,
    marks_unit, kern, kern_t, unit, weighted, stats, side, means,
    side_out, side_in, side_stats_out, side_stats, side_b, shifts,
    image_out, pair_in, line_out, line_in, norms, group_norms,
    row_sems, stat_sems, grp_sems, img_sems, norm_sems,
):
    own, width = emb_ref.shape
    marks = marks_ref.shape[0]
    vecs = vec_ref.shape[1]
    part = marks // groups
    line = members // 2
    total_rows = own * groups * members
    me_g = lax.axis_index("grp")
    me_l = lax.axis_index("lm")
    z = me_l // 2
    c = me_l % 2
    sends = []

    def to(src, dst, send_sem, recv_sem, **device):
        copy = pltpu.make_async_remote_copy(
            src_ref=src, dst_ref=dst, send_sem=send_sem, recv_sem=recv_sem,
            device_id=device, device_id_type=pl.DeviceIdType.MESH,
        )
        copy.start()
        sends.append(copy)

    def arrived(ref, sem):
        pltpu.make_async_remote_copy(
            src_ref=ref, dst_ref=ref, send_sem=sem, recv_sem=sem,
            device_id={"lm": me_l}, device_id_type=pl.DeviceIdType.MESH,
        ).wait_recv()

    def mate():
        return z * 2 + 1 - c

    def along(k):
        return (z + k) % line * 2 + c

    def group(j):
        return (me_g + j) % groups

    order = sorted(range(1, line), key=lambda k: min(k, line - k))

    barrier = pltpu.get_barrier_semaphore()
    for k in range(1, members):
        pl.semaphore_signal(
            barrier, inc=1, device_id={"lm": (me_l + k) % members},
            device_id_type=pl.DeviceIdType.MESH,
        )
    for j in range(1, groups):
        pl.semaphore_signal(
            barrier, inc=1, device_id={"grp": group(j)}, device_id_type=pl.DeviceIdType.MESH
        )

    gamma = spread_ref[0]
    weight_row = weight_ref[...]
    weight = jnp.transpose(jnp.broadcast_to(weight_row, (128, own)))[:, :1]
    values = emb_ref[...].astype(F32)
    scale = lax.rsqrt(jnp.sum(values * values, axis=1, keepdims=True) + 1e-06)
    unit[0] = (values * scale).astype(BF16)
    full = weight * vec_ref[...]
    weighted[0, 0:own, :] = full.astype(BF16)
    stats[0, 0] = jnp.zeros(stats.shape[2:], F32)
    stats[0, 0, 0:1, 0:own] = weight_row
    stats[0, 0, 1:2, 0:vecs] = jnp.sum(full, axis=0, keepdims=True)

    pl.semaphore_wait(barrier, members - 1 + groups - 1)

    def chunk(step, slot):
        pieces = [
            (weighted.at[step, pl.ds(slot * own, own), :], row_sems.at[step, 1]),
            (stats.at[step, slot], row_sems.at[step, 2]),
        ]
        if step == 0:
            pieces.insert(0, (unit.at[slot], row_sems.at[step, 0]))
        return pieces

    def spread_chunk(step):
        for (src, sem), (dst, _) in zip(chunk(step, 0), chunk(step, line)):
            to(src, dst, sem.at[1, 0], sem.at[0, line], lm=mate())
        for k in order:
            back = line - k
            for (src, sem), (dst, _) in zip(chunk(step, 0), chunk(step, back)):
                to(src, dst, sem.at[1, k], sem.at[0, back], lm=along(k))

    def pass_on(step, k):
        for (src, sem), (dst, _) in zip(chunk(step, k), chunk(step, line + k)):
            to(src, dst, sem.at[1, line + k], sem.at[0, line + k], lm=mate())

    def await_chunk(step, slot):
        for ref, sem in chunk(step, slot):
            arrived(ref, sem.at[0, slot])

    spread_chunk(0)

    mark_tile = tile(part, 256)

    for j in range(groups):
        base = group(j) * part

        def unit_marks(i, carry, j=j, base=base):
            block = marks_ref[
                pl.ds(pl.multiple_of(base + i * mark_tile, mark_tile), mark_tile), :
            ].astype(F32)
            factor = lax.rsqrt(jnp.sum(block * block, axis=1, keepdims=True) + 1e-06)
            at = pl.ds(pl.multiple_of(j * part + i * mark_tile, mark_tile), mark_tile)
            marks_unit[at, :] = (block * factor).astype(BF16)
            return carry

        lax.fori_loop(0, part // mark_tile, unit_marks, 0)

    def build(slot):
        first = slot == 0
        here = pl.ds(slot * own, own)

        def visit(i, carry):
            at = rows_at(i, mark_tile)
            block = marks_unit[at, :]
            rows = unit[slot]
            tall = jnp.exp(gamma * nt(block, rows))
            tall_b = tall.astype(BF16)
            kern_t[at, here] = tall_b
            scaled = tall * stats[0, slot, 0:1, 0:own]
            fold = scaled[:, 0:128]
            for piece in range(1, own // 128):
                fold = fold + scaled[:, piece * 128 : (piece + 1) * 128]
            product = nn(tall_b, weighted[0, here, :])
            if first:
                means[at, :] = fold
                side[at, :] = product
            else:
                means[at, :] += fold
                side[at, :] += product
            kern[here, at] = jnp.exp(gamma * nt(rows, block)).astype(BF16)
            return carry

        lax.fori_loop(0, marks // mark_tile, visit, 0)

    build(0)
    await_chunk(0, line)
    build(line)
    for k in order:
        await_chunk(0, line - k)
        pass_on(0, line - k)
        build(line - k)
        await_chunk(0, 2 * line - k)
        build(2 * line - k)

    weight_sum = jnp.zeros((1, 1), F32)
    for slot in range(members):
        weight_sum = weight_sum + jnp.sum(stats[0, slot, 0:1, 0:own], axis=1, keepdims=True)

    def average(i, carry):
        at = rows_at(i, mark_tile)
        total = jnp.sum(means[at, :], axis=1, keepdims=True) / weight_sum
        means[at, :] = jnp.broadcast_to(total, (mark_tile, 128))
        return carry

    lax.fori_loop(0, marks // mark_tile, average, 0)

    line_tile = tile(own, 256)
    gaps = None
    mean_row = None
    image = None
    for step in range(ITERS):
        totals = stats[step, 0, 1:2, 0:vecs]
        squares = stats[step, 0, 2:3, 0:vecs]
        for slot in range(1, members):
            totals = totals + stats[step, slot, 1:2, 0:vecs]
            squares = squares + stats[step, slot, 2:3, 0:vecs]

        for j in [*range(1, groups), 0]:
            def centre(i, carry, j=j):
                at = pl.ds(pl.multiple_of(j * part + i * mark_tile, mark_tile), mark_tile)
                if step == 0:
                    product = side[at, :]
                else:
                    product = nn(kern_t[at, :], weighted[step])
                product = product - means[at, 0:1] * totals
                if j == 0:
                    side[at, :] = product
                else:
                    side_out[step, j, rows_at(i, mark_tile), :] = product.astype(BF16)
                return carry

            lax.fori_loop(0, part // mark_tile, centre, 0)
            side_stats_out[step, j] = jnp.zeros(side_stats_out.shape[2:], F32)
            if step == 0:
                side_stats_out[step, j, 0:1, 0:part] = jnp.transpose(
                    means[j * part : (j + 1) * part, :]
                )[0:1, :]
                side_stats_out[step, j, 1:2, 0:128] = jnp.broadcast_to(weight_sum, (1, 128))
            side_stats_out[step, j, 2:3, 0:vecs] = totals
            side_stats_out[step, j, 3:4, 0:vecs] = squares
            if j:
                back = groups - j
                to(
                    side_stats_out.at[step, j], side_stats.at[step, back],
                    grp_sems.at[step, 0, 1, j], grp_sems.at[step, 0, 0, back], grp=group(j),
                )
                to(
                    side_out.at[step, j], side_in.at[step, back],
                    grp_sems.at[step, 1, 1, j], grp_sems.at[step, 1, 0, back], grp=group(j),
                )
        said = [side_stats_out[step, 0]]
        for j in range(1, groups):
            arrived(side_stats.at[step, j], grp_sems.at[step, 0, 0, j])
            said.append(side_stats[step, j])
        if step == 0:
            all_weight = sum(s[1:2, 0:1] for s in said)
            mean_row = sum(s[0:1, 0:part] * (s[1:2, 0:1] / all_weight) for s in said)
            gaps = [s[0:1, 0:part] - mean_row for s in said]
            factor = None
        else:
            factor = 1.0 / jnp.sqrt(sum(s[3:4, 0:vecs] for s in said) / total_rows + 1e-06)
        pad = -groups % 8
        left = gaps + [jnp.zeros_like(gaps[0])] * pad
        right = [s[2:3, 0:vecs] for s in said]
        right = right + [jnp.zeros_like(right[0])] * pad
        correction = lax.dot_general(
            jnp.concatenate(left, axis=0), jnp.concatenate(right, axis=0),
            (((0,), (0,)), ((), ())), precision=HIGHEST, preferred_element_type=F32,
        )
        summed = side[0:part, :] + correction
        for j in range(1, groups):
            arrived(side_in.at[step, j], grp_sems.at[step, 1, 0, j])
            summed = summed + side_in[step, j].astype(F32)
        if factor is not None:
            summed = summed * factor
        rounded = summed.astype(BF16)
        side_b[step, 0:part, :] = rounded
        shift = jnp.dot(
            jnp.broadcast_to(mean_row, (8, part)), rounded.astype(F32),
            precision=HIGHEST, preferred_element_type=F32,
        )
        shifts[step, 0] = shift
        for j in range(1, groups):
            back = groups - j
            to(
                shifts.at[step, 0], shifts.at[step, back],
                grp_sems.at[step, 2, 1, j], grp_sems.at[step, 2, 0, back], grp=group(j),
            )
            to(
                side_b.at[step, pl.ds(0, part), :], side_b.at[step, pl.ds(back * part, part), :],
                grp_sems.at[step, 3, 1, j], grp_sems.at[step, 3, 0, back], grp=group(j),
            )
        for j in range(1, groups):
            arrived(shifts.at[step, j], grp_sems.at[step, 2, 0, j])
            shift = shift + shifts[step, j]
            arrived(
                side_b.at[step, pl.ds(j * part, part), :], grp_sems.at[step, 3, 0, j]
            )
        shift = shift[0:1, :]

        def product(slot):
            return nn(kern[slot * own : (slot + 1) * own, :], side_b[step]) - shift

        for k in [*order, 0]:
            image_out[step, k] = product(line + k).astype(BF16)
            to(
                image_out.at[step, k], pair_in.at[step, k],
                img_sems.at[step, 0, 1, k], img_sems.at[step, 0, 0, k], lm=mate(),
            )
        for k in order:
            mine = product(k)
            arrived(pair_in.at[step, k], img_sems.at[step, 0, 0, k])
            line_out[step, k] = (mine + pair_in[step, k].astype(F32)).astype(BF16)
            to(
                line_out.at[step, k], line_in.at[step, line - k],
                img_sems.at[step, 1, 1, k], img_sems.at[step, 1, 0, line - k], lm=along(k),
            )
        image = product(0)
        arrived(pair_in.at[step, 0], img_sems.at[step, 0, 0, 0])
        image = image + pair_in[step, 0].astype(F32)
        for k in order:
            arrived(line_in.at[step, line - k], img_sems.at[step, 1, 0, line - k])
            image = image + line_in[step, line - k].astype(F32)
        image = weight * image
        square = jnp.sum(image * image, axis=0, keepdims=True)
        if step < ITERS - 1:
            full = weight * image
            weighted[step + 1, 0:own, :] = full.astype(BF16)
            stats[step + 1, 0, 1:2, 0:vecs] = jnp.sum(full, axis=0, keepdims=True)
            stats[step + 1, 0, 2:3, 0:vecs] = square
            spread_chunk(step + 1)
            for k in order:
                await_chunk(step + 1, line - k)
                pass_on(step + 1, line - k)
            await_chunk(step + 1, line)
            for k in order:
                await_chunk(step + 1, 2 * line - k)

    norms[0] = jnp.broadcast_to(square, norms.shape[1:])
    for k in range(1, members):
        back = members - k
        to(
            norms.at[0], norms.at[back], norm_sems.at[1, k], norm_sems.at[0, back],
            lm=(me_l + k) % members,
        )
    for k in range(1, members):
        arrived(norms.at[k], norm_sems.at[0, k])
        square = square + norms[k, 0:1, :]
    group_norms[0] = jnp.broadcast_to(square, norms.shape[1:])
    for j in range(1, groups):
        back = groups - j
        to(
            group_norms.at[0], group_norms.at[back],
            norm_sems.at[1, members + j], norm_sems.at[0, members + back], grp=group(j),
        )
    for j in range(1, groups):
        arrived(group_norms.at[j], norm_sems.at[0, members + j])
        square = square + group_norms[j, 0:1, :]
    out_ref[...] = image / jnp.sqrt(square / total_rows + 1e-06)
    for copy in sends:
        copy.wait_send()


def local(groups, members, embeddings, landmarks, start_vectors, row_weight, spread):
    own, width = embeddings.shape
    marks = landmarks.shape[0]
    vecs = start_vectors.shape[1]
    rows = own * members
    part = marks // groups
    line = members // 2
    wide = max(own, vecs)
    span = max(part, vecs)
    vmem = pl.BlockSpec(memory_space=pltpu.VMEM)
    dma = pltpu.SemaphoreType.DMA
    return pl.pallas_call(
        functools.partial(kernel, groups, members),
        out_shape=jax.ShapeDtypeStruct((own, vecs), F32),
        in_specs=[pl.BlockSpec(memory_space=pltpu.SMEM), vmem, vmem, vmem, vmem],
        out_specs=vmem,
        scratch_shapes=[
            pltpu.VMEM((marks, width), BF16),
            pltpu.VMEM((rows, marks), BF16),
            pltpu.VMEM((marks, rows), BF16),
            pltpu.VMEM((members, own, width), BF16),
            pltpu.VMEM((ITERS, rows, vecs), BF16),
            pltpu.VMEM((ITERS, members, 8, wide), F32),
            pltpu.VMEM((marks, vecs), F32),
            pltpu.VMEM((marks, 128), F32),
            pltpu.VMEM((ITERS, groups, part, vecs), BF16),
            pltpu.VMEM((ITERS, groups, part, vecs), BF16),
            pltpu.VMEM((ITERS, groups, 8, span), F32),
            pltpu.VMEM((ITERS, groups, 8, span), F32),
            pltpu.VMEM((ITERS, marks, vecs), BF16),
            pltpu.VMEM((ITERS, groups, 8, vecs), F32),
            pltpu.VMEM((ITERS, line, own, vecs), BF16),
            pltpu.VMEM((ITERS, line, own, vecs), BF16),
            pltpu.VMEM((ITERS, line, own, vecs), BF16),
            pltpu.VMEM((ITERS, line, own, vecs), BF16),
            pltpu.VMEM((members, 8, vecs), F32),
            pltpu.VMEM((groups, 8, vecs), F32),
            dma((ITERS, 3, 2, members)),
            dma((1,)),
            dma((ITERS, 4, 2, groups)),
            dma((ITERS, 2, 2, line)),
            dma((2, members + groups)),
        ],
        compiler_params=pltpu.CompilerParams(
            collective_id=0, has_side_effects=True, vmem_limit_bytes=62 * 2**20
        ),
    )(spread, embeddings, landmarks, start_vectors, row_weight.reshape(1, own))


def solution(mesh):
    groups, members = mesh.shape["grp"], mesh.shape["lm"]
    in_specs = (
        P(("grp", "lm"), None),
        P("lm", None),
        P(("grp", "lm"), None),
        P(("grp", "lm")),
        P(),
    )
    return jax.shard_map(
        functools.partial(local, groups, members), mesh=mesh, in_specs=in_specs,
        out_specs=P(("grp", "lm"), None), check_vma=False,
    )
```

```python
import functools

import jax
import jax.numpy as jnp
from jax import lax
from jax.experimental import pallas as pl
from jax.experimental.pallas import tpu as pltpu
from jax.sharding import PartitionSpec as P

ITERS = 2
F32 = jnp.float32
BF16 = jnp.bfloat16
BUILD = 1024
HIGHEST = lax.Precision.HIGHEST


def nt(a, b):
    return lax.dot_general(a, b, (((1,), (1,)), ((), ())), preferred_element_type=F32)


def nn(a, b):
    return jnp.dot(a, b, preferred_element_type=F32)


def tile(total, most):
    size = min(total, most)
    while total % size:
        size -= 8
    return size


def rows_at(index, size):
    return pl.ds(pl.multiple_of(index * size, size), size)


def kernel(
    groups, members, spread_ref, emb_ref, marks_ref, vec_ref, weight_ref, out_ref,
    marks_in, marks_unit, kern_t, unit, weighted, stats, side, means,
    side_out, side_in, side_stats_out, side_stats, side_b, shifts,
    image_out, pair_in, line_out, line_in, norms, group_norms,
    row_sems, stat_sems, grp_sems, img_sems, norm_sems, mark_sems, grown,
):
    own, width = emb_ref.shape
    marks = marks_ref.shape[0]
    vecs = vec_ref.shape[1]
    part = marks // groups
    line = members // 2
    total_rows = own * groups * members
    me_g = lax.axis_index("grp")
    me_l = lax.axis_index("lm")
    z = me_l // 2
    c = me_l % 2
    sends = []
    half = own // 2

    def to(src, dst, send_sem, recv_sem, when=None, **device):
        copy = pltpu.make_async_remote_copy(
            src_ref=src, dst_ref=dst, send_sem=send_sem, recv_sem=recv_sem,
            device_id=device, device_id_type=pl.DeviceIdType.MESH,
        )
        if when is None:
            copy.start()
        else:
            pl.when(when)(copy.start)
        sends.append((when, copy))

    def arrived(ref, sem):
        pltpu.make_async_remote_copy(
            src_ref=ref, dst_ref=ref, send_sem=sem, recv_sem=sem,
            device_id={"lm": me_l}, device_id_type=pl.DeviceIdType.MESH,
        ).wait_recv()

    def mate():
        return z * 2 + 1 - c

    def along(k):
        return (z + k) % line * 2 + c

    def group(j):
        return (me_g + j) % groups

    order = sorted(range(1, line), key=lambda k: min(k, line - k))

    barrier = pltpu.get_barrier_semaphore()
    for k in range(1, members):
        pl.semaphore_signal(
            barrier, inc=1, device_id={"lm": (me_l + k) % members},
            device_id_type=pl.DeviceIdType.MESH,
        )
    for j in range(1, groups):
        pl.semaphore_signal(
            barrier, inc=1, device_id={"grp": group(j)}, device_id_type=pl.DeviceIdType.MESH
        )

    mark_copies = []
    for j in range(groups):
        mark_copies.append(pltpu.make_async_copy(
            marks_ref.at[pl.ds(pl.multiple_of(group(j) * part, part), part), :],
            marks_in.at[pl.ds(j * part, part), :], mark_sems.at[j],
        ))
        mark_copies[j].start()

    gamma = spread_ref[0]
    weight_row = weight_ref[...]
    weight = jnp.transpose(jnp.broadcast_to(weight_row, (128, own)))[:, :1]
    values = emb_ref[...].astype(F32)
    scale = lax.rsqrt(jnp.sum(values * values, axis=1, keepdims=True) + 1e-06)
    unit[0] = (values * scale).astype(BF16)
    pl.semaphore_wait(barrier, members - 1 + groups - 1)

    def chunk(step, slot):
        pieces = [
            (weighted.at[step, pl.ds(slot * own, own), :], row_sems.at[step, 1]),
            (stats.at[step, slot], row_sems.at[step, 2]),
        ]
        if step == 0:
            pieces = [
                (unit.at[slot, pl.ds(0, half), :], row_sems.at[step, 0]),
                (unit.at[slot, pl.ds(half, half), :], row_sems.at[step, 3]),
            ] + pieces
        return pieces

    def chunk_at(slot):
        return [
            (unit.at[slot, pl.ds(0, half), :], row_sems.at[0, 0]),
            (unit.at[slot, pl.ds(half, half), :], row_sems.at[0, 3]),
            (weighted.at[0, pl.ds(pl.multiple_of(slot * own, own), own), :], row_sems.at[0, 1]),
            (stats.at[0, slot], row_sems.at[0, 2]),
        ]

    def send_own(low, high):
        for right in (1, 0):
            slot = line - 1 if right else 1
            pieces = zip(chunk(0, 0)[low:high], chunk(0, slot)[low:high])
            for (src, sem), (dst, _) in pieces:
                to(
                    src, dst, sem.at[1, right * line], sem.at[0, slot],
                    when=z < line - 1 if right else z > 0,
                    lm=(z + 1 if right else z - 1) * 2 + c,
                )
        for (src, sem), (dst, _) in zip(chunk(0, 0)[low:high], chunk(0, line)[low:high]):
            to(src, dst, sem.at[2, 0], sem.at[0, line], lm=mate())

    def next_slot(t):
        both = jnp.minimum(z, line - 1 - z)
        near = t < 2 * both
        far = jnp.where(near, t // 2 + 1, t - both + 1)
        left = jnp.where(near, t % 2, jnp.where(2 * z < line - 1, 1, 0)) == 0
        return jnp.where(left, line - far, far), left

    def relay(t):
        slot, left = next_slot(t)
        beyond = jnp.where(left, slot - 1, slot + 1)
        more = jnp.where(left, z < line - 1, z > 0)
        follow = jnp.where(more, beyond, slot)
        for (src, sem), (dst, _) in zip(chunk_at(slot), chunk_at(follow)):
            arrived(src, sem.at[0, slot])
            to(
                src, dst, sem.at[1, slot + jnp.where(left, line, 0)], sem.at[0, follow],
                when=more, lm=jnp.where(left, z + 1, z - 1) % line * 2 + c,
            )
        for (src, sem), (dst, _) in zip(chunk_at(slot), chunk_at(line + slot)):
            to(src, dst, sem.at[2, slot], sem.at[0, line + slot], lm=mate())
        return slot

    def spread_chunk(step):
        for (src, sem), (dst, _) in zip(chunk(step, 0), chunk(step, line)):
            to(src, dst, sem.at[1, 0], sem.at[0, line], lm=mate())
        for k in order:
            back = line - k
            for (src, sem), (dst, _) in zip(chunk(step, 0), chunk(step, back)):
                to(src, dst, sem.at[1, k], sem.at[0, back], lm=along(k))

    def pass_on(step, k):
        for (src, sem), (dst, _) in zip(chunk(step, k), chunk(step, line + k)):
            to(src, dst, sem.at[1, line + k], sem.at[0, line + k], lm=mate())

    def await_chunk(step, slot):
        for ref, sem in chunk(step, slot):
            arrived(ref, sem.at[0, slot])

    send_own(0, 2)
    full = weight * vec_ref[...]
    weighted[0, 0:own, :] = full.astype(BF16)
    stats[0, 0] = jnp.zeros(stats.shape[2:], F32)
    stats[0, 0, 0:1, 0:own] = weight_row
    stats[0, 0, 1:2, 0:vecs] = jnp.sum(full, axis=0, keepdims=True)

    send_own(2, 4)

    mark_tile = tile(part, 256)

    def unit_marks(i, carry):
        at = rows_at(i, mark_tile)
        block = marks_in[at, :].astype(F32)
        factor = lax.rsqrt(jnp.sum(block * block, axis=1, keepdims=True) + 1e-06)
        marks_unit[at, :] = (block * factor).astype(BF16)
        return carry

    for j in range(groups):
        mark_copies[j].wait()
        lax.fori_loop(
            j * part // mark_tile, (j + 1) * part // mark_tile, unit_marks, 0
        )

    def build(slot, first=False):
        here = pl.ds(pl.multiple_of(slot * own, own), own)

        def visit(i, carry):
            at = rows_at(i, build_tile)
            tall = jnp.exp(gamma * nt(marks_unit[at, :], unit[slot]))
            tall_b = tall.astype(BF16)
            kern_t[at, here] = tall_b
            scaled = tall * stats[0, slot, 0:1, 0:own]
            fold = scaled[:, 0:128]
            for piece in range(1, own // 128):
                fold = fold + scaled[:, piece * 128 : (piece + 1) * 128]
            product = nn(tall_b, weighted[0, here, :])
            if first:
                means[at, :] = fold
                side[at, :] = product
            else:
                means[at, :] += fold
                side[at, :] += product
            return carry

        lax.fori_loop(0, marks // build_tile, visit, 0)

    build_tile = tile(marks, BUILD)
    build(0, True)
    await_chunk(0, line)
    build(line)
    for t in range(line - 1):
        slot = relay(t)
        build(slot)
        for ref, sem in chunk_at(line + slot):
            arrived(ref, sem.at[0, line + slot])
        build(line + slot)

    weight_sum = jnp.zeros((1, 1), F32)
    for slot in range(members):
        weight_sum = weight_sum + jnp.sum(stats[0, slot, 0:1, 0:own], axis=1, keepdims=True)

    def average(i, carry):
        at = rows_at(i, mark_tile)
        total = jnp.sum(means[at, :], axis=1, keepdims=True) / weight_sum
        means[at, :] = jnp.broadcast_to(total, (mark_tile, 128))
        return carry

    lax.fori_loop(0, marks // mark_tile, average, 0)

    def gather_term(step, slot):
        def visit(i, carry):
            at = rows_at(i, build_tile)
            product = nn(
                kern_t[at, slot * own : (slot + 1) * own],
                weighted[step, slot * own : (slot + 1) * own, :],
            )
            side[at, :] = product if slot == 0 else side[at, :] + product
            return carry

        lax.fori_loop(0, marks // build_tile, visit, 0)

    gaps = None
    mean_row = None
    image = None
    for step in range(ITERS):
        totals = stats[step, 0, 1:2, 0:vecs]
        squares = stats[step, 0, 2:3, 0:vecs]
        for slot in range(1, members):
            totals = totals + stats[step, slot, 1:2, 0:vecs]
            squares = squares + stats[step, slot, 2:3, 0:vecs]

        for j in [*range(1, groups), 0]:
            def centre(i, carry, j=j):
                at = pl.ds(pl.multiple_of(j * part + i * mark_tile, mark_tile), mark_tile)
                product = side[at, :] - means[at, 0:1] * totals
                if j == 0:
                    side[at, :] = product
                else:
                    side_out[step, j, rows_at(i, mark_tile), :] = product.astype(BF16)
                return carry

            lax.fori_loop(0, part // mark_tile, centre, 0)
            side_stats_out[step, j] = jnp.zeros(side_stats_out.shape[2:], F32)
            if step == 0:
                side_stats_out[step, j, 0:1, 0:part] = jnp.transpose(
                    means[j * part : (j + 1) * part, :]
                )[0:1, :]
                side_stats_out[step, j, 1:2, 0:128] = jnp.broadcast_to(weight_sum, (1, 128))
            side_stats_out[step, j, 2:3, 0:vecs] = totals
            side_stats_out[step, j, 3:4, 0:vecs] = squares
            if j:
                back = groups - j
                to(
                    side_stats_out.at[step, j], side_stats.at[step, back],
                    grp_sems.at[step, 0, 1, j], grp_sems.at[step, 0, 0, back], grp=group(j),
                )
                to(
                    side_out.at[step, j], side_in.at[step, back],
                    grp_sems.at[step, 1, 1, j], grp_sems.at[step, 1, 0, back], grp=group(j),
                )
        said = [side_stats_out[step, 0]]
        for j in range(1, groups):
            arrived(side_stats.at[step, j], grp_sems.at[step, 0, 0, j])
            said.append(side_stats[step, j])
        if step == 0:
            all_weight = sum(s[1:2, 0:1] for s in said)
            mean_row = sum(s[0:1, 0:part] * (s[1:2, 0:1] / all_weight) for s in said)
            gaps = [s[0:1, 0:part] - mean_row for s in said]
            factor = None
        else:
            factor = 1.0 / jnp.sqrt(sum(s[3:4, 0:vecs] for s in said) / total_rows + 1e-06)
        pad = -groups % 8
        left = gaps + [jnp.zeros_like(gaps[0])] * pad
        right = [s[2:3, 0:vecs] for s in said]
        right = right + [jnp.zeros_like(right[0])] * pad
        correction = lax.dot_general(
            jnp.concatenate(left, axis=0), jnp.concatenate(right, axis=0),
            (((0,), (0,)), ((), ())), precision=HIGHEST, preferred_element_type=F32,
        )
        summed = side[0:part, :] + correction
        for j in range(1, groups):
            arrived(side_in.at[step, j], grp_sems.at[step, 1, 0, j])
            summed = summed + side_in[step, j].astype(F32)
        if factor is not None:
            summed = summed * factor
        rounded = summed.astype(BF16)
        side_b[step, 0] = jnp.transpose(summed).astype(BF16)
        shift = jnp.dot(
            jnp.broadcast_to(mean_row, (8, part)), rounded.astype(F32),
            precision=HIGHEST, preferred_element_type=F32,
        )
        shifts[step, 0] = shift
        for j in range(1, groups):
            back = groups - j
            to(
                shifts.at[step, 0], shifts.at[step, back],
                grp_sems.at[step, 2, 1, j], grp_sems.at[step, 2, 0, back], grp=group(j),
            )
            to(
                side_b.at[step, 0], side_b.at[step, back],
                grp_sems.at[step, 3, 1, j], grp_sems.at[step, 3, 0, back], grp=group(j),
            )
        def term(j, slot):
            block = kern_t[j * part : (j + 1) * part, slot * own : (slot + 1) * own]
            return nn(side_b[step, j], block)

        for j in range(groups):
            if j:
                arrived(shifts.at[step, j], grp_sems.at[step, 2, 0, j])
                shift = shift + shifts[step, j]
                arrived(side_b.at[step, j], grp_sems.at[step, 3, 0, j])
            if j < groups - 1:
                for slot in range(members):
                    if j == 0:
                        grown[slot] = term(j, slot)
                    else:
                        grown[slot] += term(j, slot)
        shift = jnp.transpose(jnp.broadcast_to(shift[0:1, :], (128, vecs)))[:, 0:1]

        def product(slot):
            last = term(groups - 1, slot) - shift
            return last if groups == 1 else grown[slot] + last

        for k in [*order, 0]:
            image_out[step, k] = product(line + k).astype(BF16)
            to(
                image_out.at[step, k], pair_in.at[step, k],
                img_sems.at[step, 0, 1, k], img_sems.at[step, 0, 0, k], lm=mate(),
            )
        for k in order:
            mine = product(k)
            arrived(pair_in.at[step, k], img_sems.at[step, 0, 0, k])
            line_out[step, k] = (mine + pair_in[step, k].astype(F32)).astype(BF16)
            to(
                line_out.at[step, k], line_in.at[step, line - k],
                img_sems.at[step, 1, 1, k], img_sems.at[step, 1, 0, line - k], lm=along(k),
            )
        image = product(0)
        arrived(pair_in.at[step, 0], img_sems.at[step, 0, 0, 0])
        image = image + pair_in[step, 0].astype(F32)
        for k in order:
            arrived(line_in.at[step, line - k], img_sems.at[step, 1, 0, line - k])
            image = image + line_in[step, line - k].astype(F32)
        image = weight * jnp.transpose(image)
        square = jnp.sum(image * image, axis=0, keepdims=True)
        if step < ITERS - 1:
            full = weight * image
            weighted[step + 1, 0:own, :] = full.astype(BF16)
            stats[step + 1, 0, 1:2, 0:vecs] = jnp.sum(full, axis=0, keepdims=True)
            stats[step + 1, 0, 2:3, 0:vecs] = square
            spread_chunk(step + 1)
            gather_term(step + 1, 0)
            await_chunk(step + 1, line)
            gather_term(step + 1, line)
            for k in order:
                await_chunk(step + 1, line - k)
                pass_on(step + 1, line - k)
                gather_term(step + 1, line - k)
            for k in order:
                await_chunk(step + 1, 2 * line - k)
                gather_term(step + 1, 2 * line - k)

    norms[0] = jnp.broadcast_to(square, norms.shape[1:])
    for k in range(1, members):
        back = members - k
        to(
            norms.at[0], norms.at[back], norm_sems.at[1, k], norm_sems.at[0, back],
            lm=(me_l + k) % members,
        )
    for k in range(1, members):
        arrived(norms.at[k], norm_sems.at[0, k])
        square = square + norms[k, 0:1, :]
    group_norms[0] = jnp.broadcast_to(square, norms.shape[1:])
    for j in range(1, groups):
        back = groups - j
        to(
            group_norms.at[0], group_norms.at[back],
            norm_sems.at[1, members + j], norm_sems.at[0, members + back], grp=group(j),
        )
    for j in range(1, groups):
        arrived(group_norms.at[j], norm_sems.at[0, members + j])
        square = square + group_norms[j, 0:1, :]
    out_ref[...] = image / jnp.sqrt(square / total_rows + 1e-06)
    for when, copy in sends:
        if when is None:
            copy.wait_send()
        else:
            pl.when(when)(copy.wait_send)


def local(groups, members, embeddings, landmarks, start_vectors, row_weight, spread):
    own, width = embeddings.shape
    marks = landmarks.shape[0]
    vecs = start_vectors.shape[1]
    rows = own * members
    part = marks // groups
    line = members // 2
    wide = max(own, vecs)
    span = max(part, vecs)
    vmem = pl.BlockSpec(memory_space=pltpu.VMEM)
    dma = pltpu.SemaphoreType.DMA
    return pl.pallas_call(
        functools.partial(kernel, groups, members),
        out_shape=jax.ShapeDtypeStruct((own, vecs), F32),
        in_specs=[pl.BlockSpec(memory_space=pltpu.SMEM), vmem, pl.BlockSpec(memory_space=pl.ANY), vmem, vmem],
        out_specs=vmem,
        scratch_shapes=[
            pltpu.VMEM((marks, width), BF16),
            pltpu.VMEM((marks, width), BF16),
            pltpu.VMEM((marks, rows), BF16),
            pltpu.VMEM((members, own, width), BF16),
            pltpu.VMEM((ITERS, rows, vecs), BF16),
            pltpu.VMEM((ITERS, members, 8, wide), F32),
            pltpu.VMEM((marks, vecs), F32),
            pltpu.VMEM((marks, 128), F32),
            pltpu.VMEM((ITERS, groups, part, vecs), BF16),
            pltpu.VMEM((ITERS, groups, part, vecs), BF16),
            pltpu.VMEM((ITERS, groups, 8, span), F32),
            pltpu.VMEM((ITERS, groups, 8, span), F32),
            pltpu.VMEM((ITERS, groups, vecs, part), BF16),
            pltpu.VMEM((ITERS, groups, 8, vecs), F32),
            pltpu.VMEM((ITERS, line, vecs, own), BF16),
            pltpu.VMEM((ITERS, line, vecs, own), BF16),
            pltpu.VMEM((ITERS, line, vecs, own), BF16),
            pltpu.VMEM((ITERS, line, vecs, own), BF16),
            pltpu.VMEM((members, 8, vecs), F32),
            pltpu.VMEM((groups, 8, vecs), F32),
            dma((ITERS, 4, 3, members)),
            dma((1,)),
            dma((ITERS, 4, 2, groups)),
            dma((ITERS, 2, 2, line)),
            dma((2, members + groups)),
            dma((groups,)),
            pltpu.VMEM((members, vecs, own), F32),
        ],
        compiler_params=pltpu.CompilerParams(
            collective_id=0, has_side_effects=True, vmem_limit_bytes=62 * 2**20
        ),
    )(spread, embeddings, landmarks, start_vectors, row_weight.reshape(1, own))


def solution(mesh):
    groups, members = mesh.shape["grp"], mesh.shape["lm"]
    in_specs = (
        P(("grp", "lm"), None),
        P("lm", None),
        P(("grp", "lm"), None),
        P(("grp", "lm")),
        P(),
    )
    return jax.shard_map(
        functools.partial(local, groups, members), mesh=mesh, in_specs=in_specs,
        out_specs=P(("grp", "lm"), None), check_vma=False,
    )
```

```python
import functools

import jax
import jax.numpy as jnp
from jax import lax
from jax.experimental import pallas as pl
from jax.experimental.pallas import tpu as pltpu
from jax.sharding import PartitionSpec as P

ITERS = 2
F32 = jnp.float32
BF16 = jnp.bfloat16
BUILD = 1024
HIGHEST = lax.Precision.HIGHEST


def nt(a, b):
    return lax.dot_general(a, b, (((1,), (1,)), ((), ())), preferred_element_type=F32)


def nn(a, b):
    return jnp.dot(a, b, preferred_element_type=F32)


def tile(total, most):
    size = min(total, most)
    while total % size:
        size -= 8
    return size


def rows_at(index, size):
    return pl.ds(pl.multiple_of(index * size, size), size)


def kernel(
    groups, members, spread_ref, emb_ref, marks_ref, vec_ref, weight_ref, out_ref,
    marks_in, marks_unit, kern_t, unit, weighted, stats, side, means,
    side_out, side_in, side_stats_out, side_stats, side_b, shifts,
    image_out, pair_in, line_out, line_in, norms, group_norms,
    row_sems, stat_sems, grp_sems, img_sems, norm_sems, mark_sems,
):
    own, width = emb_ref.shape
    marks = marks_ref.shape[0]
    vecs = vec_ref.shape[1]
    part = marks // groups
    line = members // 2
    total_rows = own * groups * members
    me_g = lax.axis_index("grp")
    me_l = lax.axis_index("lm")
    z = me_l // 2
    c = me_l % 2
    sends = []
    half = own // 2

    def to(src, dst, send_sem, recv_sem, when=None, **device):
        copy = pltpu.make_async_remote_copy(
            src_ref=src, dst_ref=dst, send_sem=send_sem, recv_sem=recv_sem,
            device_id=device, device_id_type=pl.DeviceIdType.MESH,
        )
        if when is None:
            copy.start()
        else:
            pl.when(when)(copy.start)
        sends.append((when, copy))

    def arrived(ref, sem):
        pltpu.make_async_remote_copy(
            src_ref=ref, dst_ref=ref, send_sem=sem, recv_sem=sem,
            device_id={"lm": me_l}, device_id_type=pl.DeviceIdType.MESH,
        ).wait_recv()

    def mate():
        return z * 2 + 1 - c

    def along(k):
        return (z + k) % line * 2 + c

    def group(j):
        return (me_g + j) % groups

    order = sorted(range(1, line), key=lambda k: min(k, line - k))

    barrier = pltpu.get_barrier_semaphore()
    for k in range(1, members):
        pl.semaphore_signal(
            barrier, inc=1, device_id={"lm": (me_l + k) % members},
            device_id_type=pl.DeviceIdType.MESH,
        )
    for j in range(1, groups):
        pl.semaphore_signal(
            barrier, inc=1, device_id={"grp": group(j)}, device_id_type=pl.DeviceIdType.MESH
        )

    mark_copies = []
    for j in range(groups):
        mark_copies.append(pltpu.make_async_copy(
            marks_ref.at[pl.ds(pl.multiple_of(group(j) * part, part), part), :],
            marks_in.at[pl.ds(j * part, part), :], mark_sems.at[j],
        ))
        mark_copies[j].start()

    gamma = spread_ref[0]
    weight_row = weight_ref[...]
    weight = jnp.transpose(jnp.broadcast_to(weight_row, (128, own)))[:, :1]
    values = emb_ref[...].astype(F32)
    scale = lax.rsqrt(jnp.sum(values * values, axis=1, keepdims=True) + 1e-06)
    unit[0] = (values * scale).astype(BF16)
    pl.semaphore_wait(barrier, members - 1 + groups - 1)

    def chunk(step, slot):
        pieces = [
            (weighted.at[step, pl.ds(slot * own, own), :], row_sems.at[step, 1]),
            (stats.at[step, slot], row_sems.at[step, 2]),
        ]
        if step == 0:
            pieces = [
                (unit.at[slot, pl.ds(0, half), :], row_sems.at[step, 0]),
                (unit.at[slot, pl.ds(half, half), :], row_sems.at[step, 3]),
            ] + pieces
        return pieces

    def chunk_at(slot):
        return [
            (unit.at[slot, pl.ds(0, half), :], row_sems.at[0, 0]),
            (unit.at[slot, pl.ds(half, half), :], row_sems.at[0, 3]),
            (weighted.at[0, pl.ds(pl.multiple_of(slot * own, own), own), :], row_sems.at[0, 1]),
            (stats.at[0, slot], row_sems.at[0, 2]),
        ]

    def send_own(low, high):
        for right in (1, 0):
            slot = line - 1 if right else 1
            pieces = zip(chunk(0, 0)[low:high], chunk(0, slot)[low:high])
            for (src, sem), (dst, _) in pieces:
                to(
                    src, dst, sem.at[1, right * line], sem.at[0, slot],
                    when=z < line - 1 if right else z > 0,
                    lm=(z + 1 if right else z - 1) * 2 + c,
                )
        for (src, sem), (dst, _) in zip(chunk(0, 0)[low:high], chunk(0, line)[low:high]):
            to(src, dst, sem.at[2, 0], sem.at[0, line], lm=mate())

    def next_slot(t):
        both = jnp.minimum(z, line - 1 - z)
        near = t < 2 * both
        far = jnp.where(near, t // 2 + 1, t - both + 1)
        left = jnp.where(near, t % 2, jnp.where(2 * z < line - 1, 1, 0)) == 0
        return jnp.where(left, line - far, far), left

    def relay(t):
        slot, left = next_slot(t)
        beyond = jnp.where(left, slot - 1, slot + 1)
        more = jnp.where(left, z < line - 1, z > 0)
        follow = jnp.where(more, beyond, slot)
        for (src, sem), (dst, _) in zip(chunk_at(slot), chunk_at(follow)):
            arrived(src, sem.at[0, slot])
            to(
                src, dst, sem.at[1, slot + jnp.where(left, line, 0)], sem.at[0, follow],
                when=more, lm=jnp.where(left, z + 1, z - 1) % line * 2 + c,
            )
        for (src, sem), (dst, _) in zip(chunk_at(slot), chunk_at(line + slot)):
            to(src, dst, sem.at[2, slot], sem.at[0, line + slot], lm=mate())
        return slot

    def spread_chunk(step):
        for (src, sem), (dst, _) in zip(chunk(step, 0), chunk(step, line)):
            to(src, dst, sem.at[1, 0], sem.at[0, line], lm=mate())
        for k in order:
            back = line - k
            for (src, sem), (dst, _) in zip(chunk(step, 0), chunk(step, back)):
                to(src, dst, sem.at[1, k], sem.at[0, back], lm=along(k))

    def pass_on(step, k):
        for (src, sem), (dst, _) in zip(chunk(step, k), chunk(step, line + k)):
            to(src, dst, sem.at[1, line + k], sem.at[0, line + k], lm=mate())

    def await_chunk(step, slot):
        for ref, sem in chunk(step, slot):
            arrived(ref, sem.at[0, slot])

    send_own(0, 2)
    full = weight * vec_ref[...]
    weighted[0, 0:own, :] = full.astype(BF16)
    stats[0, 0] = jnp.zeros(stats.shape[2:], F32)
    stats[0, 0, 0:1, 0:own] = weight_row
    stats[0, 0, 1:2, 0:vecs] = jnp.sum(full, axis=0, keepdims=True)

    send_own(2, 4)

    mark_tile = tile(part, 256)

    def unit_marks(i, carry):
        at = rows_at(i, mark_tile)
        block = marks_in[at, :].astype(F32)
        factor = lax.rsqrt(jnp.sum(block * block, axis=1, keepdims=True) + 1e-06)
        marks_unit[at, :] = (block * factor).astype(BF16)
        return carry

    for j in range(groups):
        mark_copies[j].wait()
        lax.fori_loop(
            j * part // mark_tile, (j + 1) * part // mark_tile, unit_marks, 0
        )

    def build(slot, first=False):
        here = pl.ds(pl.multiple_of(slot * own, own), own)

        def visit(i, carry):
            at = rows_at(i, build_tile)
            tall = jnp.exp(gamma * nt(marks_unit[at, :], unit[slot]))
            tall_b = tall.astype(BF16)
            kern_t[at, here] = tall_b
            scaled = tall * stats[0, slot, 0:1, 0:own]
            fold = scaled[:, 0:128]
            for piece in range(1, own // 128):
                fold = fold + scaled[:, piece * 128 : (piece + 1) * 128]
            product = nn(tall_b, weighted[0, here, :])
            if first:
                means[at, :] = fold
                side[at, :] = product
            else:
                means[at, :] += fold
                side[at, :] += product
            return carry

        lax.fori_loop(0, marks // build_tile, visit, 0)

    build_tile = tile(marks, BUILD)
    build(0, True)
    await_chunk(0, line)
    build(line)
    for t in range(line - 1):
        slot = relay(t)
        build(slot)
        for ref, sem in chunk_at(line + slot):
            arrived(ref, sem.at[0, line + slot])
        build(line + slot)

    weight_sum = jnp.zeros((1, 1), F32)
    for slot in range(members):
        weight_sum = weight_sum + jnp.sum(stats[0, slot, 0:1, 0:own], axis=1, keepdims=True)

    def average(i, carry):
        at = rows_at(i, mark_tile)
        total = jnp.sum(means[at, :], axis=1, keepdims=True) / weight_sum
        means[at, :] = jnp.broadcast_to(total, (mark_tile, 128))
        return carry

    lax.fori_loop(0, marks // mark_tile, average, 0)

    gaps = None
    mean_row = None
    image = None
    for step in range(ITERS):
        totals = stats[step, 0, 1:2, 0:vecs]
        squares = stats[step, 0, 2:3, 0:vecs]
        for slot in range(1, members):
            totals = totals + stats[step, slot, 1:2, 0:vecs]
            squares = squares + stats[step, slot, 2:3, 0:vecs]

        for j in [*range(1, groups), 0]:
            def centre(i, carry, j=j):
                at = pl.ds(pl.multiple_of(j * part + i * mark_tile, mark_tile), mark_tile)
                if step == 0:
                    product = side[at, :]
                else:
                    product = nn(kern_t[at, :], weighted[step])
                product = product - means[at, 0:1] * totals
                if j == 0:
                    side[at, :] = product
                else:
                    side_out[step, j, rows_at(i, mark_tile), :] = product.astype(BF16)
                return carry

            lax.fori_loop(0, part // mark_tile, centre, 0)
            side_stats_out[step, j] = jnp.zeros(side_stats_out.shape[2:], F32)
            if step == 0:
                side_stats_out[step, j, 0:1, 0:part] = jnp.transpose(
                    means[j * part : (j + 1) * part, :]
                )[0:1, :]
                side_stats_out[step, j, 1:2, 0:128] = jnp.broadcast_to(weight_sum, (1, 128))
            side_stats_out[step, j, 2:3, 0:vecs] = totals
            side_stats_out[step, j, 3:4, 0:vecs] = squares
            if j:
                back = groups - j
                to(
                    side_stats_out.at[step, j], side_stats.at[step, back],
                    grp_sems.at[step, 0, 1, j], grp_sems.at[step, 0, 0, back], grp=group(j),
                )
                to(
                    side_out.at[step, j], side_in.at[step, back],
                    grp_sems.at[step, 1, 1, j], grp_sems.at[step, 1, 0, back], grp=group(j),
                )
        said = [side_stats_out[step, 0]]
        for j in range(1, groups):
            arrived(side_stats.at[step, j], grp_sems.at[step, 0, 0, j])
            said.append(side_stats[step, j])
        if step == 0:
            all_weight = sum(s[1:2, 0:1] for s in said)
            mean_row = sum(s[0:1, 0:part] * (s[1:2, 0:1] / all_weight) for s in said)
            gaps = [s[0:1, 0:part] - mean_row for s in said]
            factor = None
        else:
            factor = 1.0 / jnp.sqrt(sum(s[3:4, 0:vecs] for s in said) / total_rows + 1e-06)
        pad = -groups % 8
        left = gaps + [jnp.zeros_like(gaps[0])] * pad
        right = [s[2:3, 0:vecs] for s in said]
        right = right + [jnp.zeros_like(right[0])] * pad
        correction = lax.dot_general(
            jnp.concatenate(left, axis=0), jnp.concatenate(right, axis=0),
            (((0,), (0,)), ((), ())), precision=HIGHEST, preferred_element_type=F32,
        )
        summed = side[0:part, :] + correction
        for j in range(1, groups):
            arrived(side_in.at[step, j], grp_sems.at[step, 1, 0, j])
            summed = summed + side_in[step, j].astype(F32)
        if factor is not None:
            summed = summed * factor
        rounded = summed.astype(BF16)
        side_b[step, 0] = jnp.transpose(summed).astype(BF16)
        shift = jnp.dot(
            jnp.broadcast_to(mean_row, (8, part)), rounded.astype(F32),
            precision=HIGHEST, preferred_element_type=F32,
        )
        shifts[step, 0] = shift
        for j in range(1, groups):
            back = groups - j
            to(
                shifts.at[step, 0], shifts.at[step, back],
                grp_sems.at[step, 2, 1, j], grp_sems.at[step, 2, 0, back], grp=group(j),
            )
            to(
                side_b.at[step, 0], side_b.at[step, back],
                grp_sems.at[step, 3, 1, j], grp_sems.at[step, 3, 0, back], grp=group(j),
            )
        for j in range(groups):
            if j:
                arrived(shifts.at[step, j], grp_sems.at[step, 2, 0, j])
                shift = shift + shifts[step, j]
                arrived(side_b.at[step, j], grp_sems.at[step, 3, 0, j])
        shift = jnp.transpose(jnp.broadcast_to(shift[0:1, :], (128, vecs)))[:, 0:1]

        def product(slot):
            whole = jnp.concatenate([side_b[step, j] for j in range(groups)], axis=1)
            return nn(whole, kern_t[:, slot * own : (slot + 1) * own]) - shift

        for k in [*order, 0]:
            image_out[step, k] = product(line + k).astype(BF16)
            to(
                image_out.at[step, k], pair_in.at[step, k],
                img_sems.at[step, 0, 1, k], img_sems.at[step, 0, 0, k], lm=mate(),
            )
        for k in order:
            mine = product(k)
            arrived(pair_in.at[step, k], img_sems.at[step, 0, 0, k])
            line_out[step, k] = (mine + pair_in[step, k].astype(F32)).astype(BF16)
            to(
                line_out.at[step, k], line_in.at[step, line - k],
                img_sems.at[step, 1, 1, k], img_sems.at[step, 1, 0, line - k], lm=along(k),
            )
        image = product(0)
        arrived(pair_in.at[step, 0], img_sems.at[step, 0, 0, 0])
        image = image + pair_in[step, 0].astype(F32)
        for k in order:
            arrived(line_in.at[step, line - k], img_sems.at[step, 1, 0, line - k])
            image = image + line_in[step, line - k].astype(F32)
        image = weight * jnp.transpose(image)
        square = jnp.sum(image * image, axis=0, keepdims=True)
        if step < ITERS - 1:
            full = weight * image
            weighted[step + 1, 0:own, :] = full.astype(BF16)
            stats[step + 1, 0, 1:2, 0:vecs] = jnp.sum(full, axis=0, keepdims=True)
            stats[step + 1, 0, 2:3, 0:vecs] = square
            spread_chunk(step + 1)
            for k in order:
                await_chunk(step + 1, line - k)
                pass_on(step + 1, line - k)
            await_chunk(step + 1, line)
            for k in order:
                await_chunk(step + 1, 2 * line - k)

    norms[0] = jnp.broadcast_to(square, norms.shape[1:])
    for k in range(1, members):
        back = members - k
        to(
            norms.at[0], norms.at[back], norm_sems.at[1, k], norm_sems.at[0, back],
            lm=(me_l + k) % members,
        )
    for k in range(1, members):
        arrived(norms.at[k], norm_sems.at[0, k])
        square = square + norms[k, 0:1, :]
    group_norms[0] = jnp.broadcast_to(square, norms.shape[1:])
    for j in range(1, groups):
        back = groups - j
        to(
            group_norms.at[0], group_norms.at[back],
            norm_sems.at[1, members + j], norm_sems.at[0, members + back], grp=group(j),
        )
    for j in range(1, groups):
        arrived(group_norms.at[j], norm_sems.at[0, members + j])
        square = square + group_norms[j, 0:1, :]
    out_ref[...] = image / jnp.sqrt(square / total_rows + 1e-06)
    for when, copy in sends:
        if when is None:
            copy.wait_send()
        else:
            pl.when(when)(copy.wait_send)


def local(groups, members, embeddings, landmarks, start_vectors, row_weight, spread):
    own, width = embeddings.shape
    marks = landmarks.shape[0]
    vecs = start_vectors.shape[1]
    rows = own * members
    part = marks // groups
    line = members // 2
    wide = max(own, vecs)
    span = max(part, vecs)
    vmem = pl.BlockSpec(memory_space=pltpu.VMEM)
    dma = pltpu.SemaphoreType.DMA
    return pl.pallas_call(
        functools.partial(kernel, groups, members),
        out_shape=jax.ShapeDtypeStruct((own, vecs), F32),
        in_specs=[pl.BlockSpec(memory_space=pltpu.SMEM), vmem, pl.BlockSpec(memory_space=pl.ANY), vmem, vmem],
        out_specs=vmem,
        scratch_shapes=[
            pltpu.VMEM((marks, width), BF16),
            pltpu.VMEM((marks, width), BF16),
            pltpu.VMEM((marks, rows), BF16),
            pltpu.VMEM((members, own, width), BF16),
            pltpu.VMEM((ITERS, rows, vecs), BF16),
            pltpu.VMEM((ITERS, members, 8, wide), F32),
            pltpu.VMEM((marks, vecs), F32),
            pltpu.VMEM((marks, 128), F32),
            pltpu.VMEM((ITERS, groups, part, vecs), BF16),
            pltpu.VMEM((ITERS, groups, part, vecs), BF16),
            pltpu.VMEM((ITERS, groups, 8, span), F32),
            pltpu.VMEM((ITERS, groups, 8, span), F32),
            pltpu.VMEM((ITERS, groups, vecs, part), BF16),
            pltpu.VMEM((ITERS, groups, 8, vecs), F32),
            pltpu.VMEM((ITERS, line, vecs, own), BF16),
            pltpu.VMEM((ITERS, line, vecs, own), BF16),
            pltpu.VMEM((ITERS, line, vecs, own), BF16),
            pltpu.VMEM((ITERS, line, vecs, own), BF16),
            pltpu.VMEM((members, 8, vecs), F32),
            pltpu.VMEM((groups, 8, vecs), F32),
            dma((ITERS, 4, 3, members)),
            dma((1,)),
            dma((ITERS, 4, 2, groups)),
            dma((ITERS, 2, 2, line)),
            dma((2, members + groups)),
            dma((groups,)),
        ],
        compiler_params=pltpu.CompilerParams(
            collective_id=0, has_side_effects=True, vmem_limit_bytes=62 * 2**20
        ),
    )(spread, embeddings, landmarks, start_vectors, row_weight.reshape(1, own))


def solution(mesh):
    groups, members = mesh.shape["grp"], mesh.shape["lm"]
    in_specs = (
        P(("grp", "lm"), None),
        P("lm", None),
        P(("grp", "lm"), None),
        P(("grp", "lm")),
        P(),
    )
    return jax.shard_map(
        functools.partial(local, groups, members), mesh=mesh, in_specs=in_specs,
        out_specs=P(("grp", "lm"), None), check_vma=False,
    )
```
